256 devices in a mesh: leaf: 32 (over x, z), sub: 8 (over y, core).
Axes of the slice: x: 4, y: 4, z: 8, core: 2. Of those that a mesh axis runs over, the one named last changes fastest.
Arguments:
- leaf_right: bfloat16 [1024, 512, 256], P(('leaf', 'sub')), may hold values from -6 to 6
- leaf_inverse: bfloat16 [1024, 512, 512], P(('leaf', 'sub')), may hold values from -2.5 to 2.5, as said below
- panels: bfloat16 [1024, 256, 512], P(('leaf', 'sub')), may hold values from -0.125 to 0.125
- leaf_subtree: int32 [1024], P(('leaf', 'sub')), may hold values from 0 to 31, as said below
- panel_block: int32 [1024, 4], P(('leaf', 'sub')), may hold values from 0 to 63
- separator_right: bfloat16 [131072, 256], P(('leaf', 'sub')), may hold values from -6 to 6
- separator_inverse: bfloat16 [131072, 512], P(('leaf', 'sub')), may hold values from -2.5 to 2.5, as said below
- separator_factor: bfloat16 [131072, 4096], P(('leaf', 'sub')), may hold values from -1 to 1, as said below
Outputs:
- leaf_solution: bfloat16 [1024, 512, 256], P(('leaf', 'sub'))
- separator_solution: bfloat16 [131072, 256], P(('leaf', 'sub'))
The draws below stay inside these ranges and needn't reach their ends.
Inputs may be any that keep to these rules, and one draw needn't show every extreme that they name: `leaf_subtree`: every leaf supernode held by section s of the leaf axis belongs to a subtree between s - (2) and s. Each device of section s holds, for every d from 0 to min(2, s), at least one leaf supernode of subtree s - d. `leaf_inverse`: each 512 x 512 block is lower triangular, with its diagonal between 0.6 and 1.4. `separator_inverse`: each 512 x 512 block is lower triangular, with its diagonal between 0.6 and 1.4. `separator_factor`: within each subtree's 4096 rows, the block of row block q and column block p (blocks of 512) is zero unless q > p.
All inputs are finite; a program needn't handle non-finite values.
Results may differ from the reference program's by a relative error of at most 0.024.
Values may be sent and summed in bfloat16 or wider, within the bound.
No kernel may reach another device: no remote copies, remote signals or barrier semaphores. Data moves between devices by JAX's collectives and lax.ppermute only.
A program may use at most 128 MiB of HBM per device.

```python
import math
import jax
import jax.numpy as jnp
from jax import lax

W = 512
WSN = 512
SA = 4096
R = 256
BLK = 64
KB = 4
SPAN = 3
SN_DEV = 4
LEAVES = 1024
NSEP = 32
NBS = 64


def triangle(key, count_blocks, width):
    rows = jnp.arange(width)
    lower = (rows[None, :] < rows[:, None]).astype(jnp.float32)
    identity_mask = (rows[None, :] == rows[:, None]).astype(jnp.float32)
    noise_key, diagonal_key = jax.random.split(key)
    noise = jnp.clip(jax.random.normal(noise_key, (count_blocks, width, width), jnp.float32), -4.0, 4.0)
    spread = 0.6 / jnp.sqrt(rows.astype(jnp.float32) + 1.0)
    diagonal = jax.random.uniform(diagonal_key, (count_blocks, width), jnp.float32, 0.6, 1.4)
    return noise * lower[None, :, :] * spread[None, :, None] + diagonal[:, :, None] * identity_mask[None, :, :]


def draw_leaf_inverse(key, part):
    return triangle(key, LEAVES, W).astype(jnp.bfloat16)


def draw_separator_inverse(key, part):
    return triangle(key, NSEP * (SA // WSN), WSN).reshape(NSEP * SA, WSN).astype(jnp.bfloat16)


def draw_separator_factor(key, part):
    rows = jnp.arange(SA)
    blocks = rows // WSN
    next_block = (blocks[:, None] == blocks[None, :] + 1).astype(jnp.float32)
    far_block = (blocks[:, None] > blocks[None, :] + 1).astype(jnp.float32)
    scale_table = (0.75 * next_block + 0.2 * far_block) / math.sqrt(WSN)

    def one_section(index):
        section_key = jax.random.fold_in(key, index)
        noise = jnp.clip(jax.random.normal(section_key, (SA, SA), jnp.float32), -4.0, 4.0)
        return (noise * scale_table).astype(jnp.bfloat16)
    return lax.map(one_section, jnp.arange(NSEP)).reshape(NSEP * SA, SA)


def draw_leaf_subtree(key, part):
    devices = LEAVES // SN_DEV
    per_section = devices // NSEP

    def one_device(index):
        device_key = jax.random.fold_in(key, index)
        first_key, rest_key, order_key = jax.random.split(device_key, 3)
        first = jax.random.permutation(first_key, SPAN)
        others = jax.random.randint(rest_key, (SN_DEV - SPAN,), 0, SPAN)
        backward = jnp.concatenate([first, others])
        section = index // per_section
        backward = jnp.minimum(backward, section)
        backward = jax.random.permutation(order_key, backward)
        return section - backward
    return jax.vmap(one_device)(jnp.arange(devices)).reshape(LEAVES).astype(jnp.int32)


def with_ends(entries, own_key, smallest, largest):
    spot = [jax.random.randint(jax.random.fold_in(own_key, axis), (), 0, length) for axis, length in enumerate(entries.shape)]
    longest = entries.shape.index(max(entries.shape))
    next_to = spot[:longest] + [(spot[longest] + 1) % entries.shape[longest]] + spot[longest + 1:]
    return entries.at[tuple(spot)].set(smallest).at[tuple(next_to)].set(largest)


def levels(stream_key, extent, cuts, least, high):
    def one(axis_at, blocks):
        draws = jax.random.uniform(jax.random.fold_in(jax.random.fold_in(stream_key, 6), axis_at), (blocks,), jnp.float32, least / len(cuts), high / len(cuts))
        return jnp.repeat(jnp.exp(draws), extent[axis_at] // blocks).reshape((-1,) + (1,) * (len(extent) - axis_at - 1))

    gain = one(*cuts[0])
    for cut in cuts[1:]:
        gain = gain * one(*cut)
    return gain


def scatter_about(own_key, extent, scale, limit, cuts=(), kind=jnp.bfloat16):
    drawn = jax.random.normal(own_key, extent, jnp.float32) * scale
    if len(cuts) > 0:
        drawn = levels(own_key, extent, cuts, -0.22, 0.18) * drawn
    return jnp.clip(drawn, min=-limit, max=limit).astype(kind)


def setup_inputs(seed: int = 0) -> dict:
    keys = jax.random.split(jax.random.key(seed), 9)
    return {
        "leaf_right": scatter_about(keys[0], (LEAVES, W, R), 1.0, 6.0, ((0, 256),)),
        "leaf_inverse": draw_leaf_inverse(jax.random.fold_in(keys[8], 71), 0),
        "panels": scatter_about(keys[2], (LEAVES, KB * BLK, W), (4 * W) ** -0.5, 0.125, ((0, 256),)),
        "leaf_subtree": draw_leaf_subtree(jax.random.fold_in(keys[8], 71), 0),
        "panel_block": with_ends(jax.random.randint(keys[4], (LEAVES, KB), 0, NBS), jax.random.fold_in(keys[4], 1), 0, NBS - 1).astype(jnp.int32),
        "separator_right": scatter_about(keys[5], (NSEP * SA, R), 1.0, 6.0, ((0, 256),)),
        "separator_inverse": draw_separator_inverse(jax.random.fold_in(keys[8], 71), 0),
        "separator_factor": draw_separator_factor(jax.random.fold_in(keys[8], 71), 0),
    }


def solve_leaves(inverse, right):
    return jnp.einsum("jab,jbr->jar", inverse.astype(jnp.float32), right.astype(jnp.float32)).astype(jnp.bfloat16)


def sweep_section(section_args):
    rhs, inverse, factor = section_args
    count = SA // WSN
    forward_blocks = []
    for column in range(count):
        first = column * WSN
        running = rhs[first:first + WSN].astype(jnp.float32)
        if column > 0:
            earlier = jnp.concatenate(forward_blocks, 0)
            running = running - jnp.dot(factor[first:first + WSN, :first], earlier, preferred_element_type=jnp.float32)
        forward_blocks.append(jnp.dot(inverse[first:first + WSN].astype(jnp.float32), running, precision=lax.Precision.HIGHEST, preferred_element_type=jnp.float32).astype(jnp.bfloat16))
    backward_blocks = [None] * count
    for column in reversed(range(count)):
        first = column * WSN
        running = forward_blocks[column].astype(jnp.float32)
        if column < count - 1:
            later = jnp.concatenate(backward_blocks[column + 1:], 0)
            running = running - lax.dot_general(factor[first + WSN:, first:first + WSN], later, (((0,), (0,)), ((), ())), preferred_element_type=jnp.float32)
        backward_blocks[column] = lax.dot_general(inverse[first:first + WSN].astype(jnp.float32), running, (((0,), (0,)), ((), ())), precision=lax.Precision.HIGHEST, preferred_element_type=jnp.float32).astype(jnp.bfloat16)
    return jnp.concatenate(backward_blocks, 0)


def reference(leaf_right, leaf_inverse, panels, leaf_subtree, panel_block, separator_right, separator_inverse, separator_factor):
    groups = leaf_right.shape[0] // SN_DEV
    row_blocks = SA // BLK
    targets_all = (leaf_subtree[:, None] * row_blocks + panel_block).astype(jnp.int32).reshape(groups, SN_DEV * KB)
    inputs = (leaf_right.reshape(groups, SN_DEV, W, R), leaf_inverse.reshape(groups, SN_DEV, W, W), panels.reshape(groups, SN_DEV, KB * BLK, W), targets_all)

    def forward_step(sums, group):
        right, inverse, panel_group, targets = group
        solved = solve_leaves(inverse, right)
        updates = jnp.einsum("jib,jbr->jir", panel_group.astype(jnp.float32), solved.astype(jnp.float32))
        return sums.at[targets].add(updates.reshape(SN_DEV * KB, BLK, R)), jnp.zeros((), jnp.float32)

    sums, unused = lax.scan(forward_step, jnp.zeros((NSEP * row_blocks, BLK, R), jnp.float32), inputs)
    separator_rhs = (separator_right.astype(jnp.float32) - sums.reshape(NSEP * SA, R)).astype(jnp.bfloat16)
    separator_x = lax.map(sweep_section, (separator_rhs.reshape(NSEP, SA, R), separator_inverse.reshape(NSEP, SA, WSN), separator_factor.reshape(NSEP, SA, SA)))
    solution_blocks = separator_x.reshape(NSEP * row_blocks, BLK, R)

    def backward_step(carry, group):
        right, inverse, panel_group, targets = group
        solved = solve_leaves(inverse, right)
        pieces = jnp.take(solution_blocks, targets, axis=0).reshape(SN_DEV, KB * BLK, R)
        reduced = jnp.einsum("jib,jir->jbr", panel_group.astype(jnp.float32), pieces.astype(jnp.float32))
        inner_rhs = (solved.astype(jnp.float32) - reduced).astype(jnp.bfloat16)
        result = jnp.einsum("jab,jar->jbr", inverse.astype(jnp.float32), inner_rhs.astype(jnp.float32)).astype(jnp.bfloat16)
        return carry, result

    unused_carry, leaf_solution = lax.scan(backward_step, jnp.zeros((), jnp.float32), inputs)
    return leaf_solution.reshape(groups * SN_DEV, W, R), separator_x.reshape(NSEP * SA, R)
```

```python
import jax
import jax.numpy as jnp
from jax import lax
from jax.experimental import pallas as pl
from jax.experimental.pallas import tpu as pltpu
from jax.sharding import PartitionSpec as P

W = 512
WSN = 512
SA = 4096
R = 256
BLK = 64
KB = 4
SPAN = 3
SN_DEV = 4
GROUP = 8
COLS = R // GROUP
CHUNKS = SA // 128
UPD = SN_DEV * KB * BLK
SEND = UPD + WSN
HUB = 3
bf16 = jnp.bfloat16
f32 = jnp.float32
NT = (((1,), (1,)), ((), ()))
NN = (((1,), (0,)), ((), ()))
MIB = 1 << 20


def dot(a, b, dims):
    return lax.dot_general(a, b, dims, preferred_element_type=f32)


def leaf_forward_kernel(right, inverse, panel, sep_right, y_out, send):
    j = pl.program_id(0)
    y = dot(right[0].T, inverse[0], NT).astype(bf16)
    y_out[0] = y
    send[:, pl.ds(pl.multiple_of(j * KB * BLK, 128), KB * BLK)] = dot(y, panel[0], NT).astype(bf16)

    @pl.when(j == 0)
    def _():
        send[:, UPD:] = sep_right[...].T


def leaf_forward(right, inverse, panels, sep_right):
    return pl.pallas_call(
        leaf_forward_kernel,
        grid=(SN_DEV,),
        in_specs=[
            pl.BlockSpec((1, W, R), lambda j: (j, 0, 0)),
            pl.BlockSpec((1, W, W), lambda j: (j, 0, 0)),
            pl.BlockSpec((1, KB * BLK, W), lambda j: (j, 0, 0)),
            pl.BlockSpec((WSN, R), lambda j: (0, 0)),
        ],
        out_specs=[
            pl.BlockSpec((1, R, W), lambda j: (j, 0, 0)),
            pl.BlockSpec((R, SEND), lambda j: (0, 0)),
        ],
        out_shape=[
            jax.ShapeDtypeStruct((SN_DEV, R, W), bf16),
            jax.ShapeDtypeStruct((R, SEND), bf16),
        ],
        compiler_params=pltpu.CompilerParams(dimension_semantics=("arbitrary",), vmem_limit_bytes=24 * MIB),
        name="leaf_forward",
    )(right, inverse, panels, sep_right)


def scatter_kernel(slots, received, base, near, far, table):
    table[...] = jnp.zeros_like(table)
    high = lax.broadcasted_iota(jnp.int32, (COLS, 128), 1) >= BLK

    def from_member(s, carry):
        for i in range(UPD // 128):
            pair = received[s, :, 128 * i : 128 * i + 128].astype(f32)
            turned = pltpu.roll(pair, BLK, 1)
            for h in range(2):
                slot = slots[16 * s + 2 * i + h]
                want_high = (slot & 1) == 1
                moved = jnp.where(want_high, turned if h == 0 else pair, pair if h == 0 else turned)
                row = slot >> 1
                table[row] = table[row] + jnp.where(high == want_high, moved, 0.0)
        return carry

    lax.fori_loop(0, GROUP, from_member, 0)
    for c in range(CHUNKS):
        first = UPD + 128 * (c % 4)
        base[c] = received[c // 4, :, first : first + 128].astype(f32) - table[c]
        near[c] = table[CHUNKS + c].astype(bf16)
        far[c] = table[2 * CHUNKS + c].astype(bf16)


def scatter(slots, received):
    share = (CHUNKS, COLS, 128)
    return pl.pallas_call(
        scatter_kernel,
        in_specs=[pl.BlockSpec(memory_space=pltpu.SMEM), pl.BlockSpec(memory_space=pltpu.VMEM)],
        out_specs=[pl.BlockSpec(memory_space=pltpu.VMEM)] * 3,
        out_shape=[
            jax.ShapeDtypeStruct(share, f32),
            jax.ShapeDtypeStruct(share, bf16),
            jax.ShapeDtypeStruct(share, bf16),
        ],
        scratch_shapes=[pltpu.VMEM((SPAN * CHUNKS, COLS, 128), f32)],
        compiler_params=pltpu.CompilerParams(vmem_limit_bytes=16 * MIB),
        name="scatter_updates",
    )(slots, received)


def sweep_kernel(where, *refs):
    rhs = refs[0:4]
    wide = refs[4:10]
    inverse = refs[10:18]
    beside = refs[18:26]
    outs = refs[26:30]
    lower, diagonal, state, lower_sem, diagonal_sem, beside_sem = refs[30:]
    core = where[1]

    def rows_of(k, same):
        q = 2 * k + (core if same else 1 - core)
        return pl.ds(pl.multiple_of(q * WSN, WSN), WSN)

    @pl.when(where[0] == HUB)
    def _():
        for k in range(4):
            for same in (0, 1):
                dst = diagonal.at[rows_of(k, same == 0)]
                pltpu.make_async_copy(inverse[2 * k + same], dst, diagonal_sem.at[k]).start()
            for same in (0, 1):

                @pl.when(core == 1 - same)
                def _():
                    dst = lower.at[(2 * k + 1) * WSN : (2 * k + 2) * WSN, 2 * k * WSN : (2 * k + 1) * WSN]
                    pltpu.make_async_copy(beside[2 * k + same], dst, beside_sem.at[k]).start()

            if k > 0:
                for same in (0, 1):
                    dst = lower.at[rows_of(k, same == 0), 0 : 2 * k * WSN]
                    pltpu.make_async_copy(wide[2 * (k - 1) + same], dst, lower_sem.at[k]).start()
        for k in range(4):
            for c in range(CHUNKS):
                state[COLS * k : COLS * k + COLS, 128 * c : 128 * c + 128] = rhs[k][c]
        for q in range(8):
            k = q // 2
            if q % 2 == 0:
                both = diagonal.at[2 * k * WSN : (2 * k + 2) * WSN]
                pltpu.make_async_copy(both, both, diagonal_sem.at[k]).wait()
                single = lower.at[(2 * k + 1) * WSN : (2 * k + 2) * WSN, 2 * k * WSN : (2 * k + 1) * WSN]
                pltpu.make_async_copy(single, single, beside_sem.at[k]).wait()
                if k > 0:
                    slab = lower.at[2 * k * WSN : (2 * k + 2) * WSN, 0 : 2 * k * WSN]
                    pltpu.make_async_copy(slab, slab, lower_sem.at[k]).wait()
            here = slice(q * WSN, (q + 1) * WSN)
            bracket = state[:, here].astype(f32)
            if q > 0:
                bracket = bracket - dot(state[:, : q * WSN], lower[here, : q * WSN], NT)
            state[:, here] = by_inverse(bracket, diagonal[here], NT)
        for q in reversed(range(8)):
            here = slice(q * WSN, (q + 1) * WSN)
            bracket = state[:, here].astype(f32)
            if q < 7:
                bracket = bracket - dot(state[:, (q + 1) * WSN :], lower[(q + 1) * WSN :, here], NN)
            solved = by_inverse(bracket, diagonal[here], NN)
            state[:, here] = solved
            for k in range(4):
                for t in range(4):
                    outs[k][4 * q + t] = solved[COLS * k : COLS * k + COLS, 128 * t : 128 * t + 128]


def by_inverse(bracket, block, dims):
    head = bracket.astype(bf16)
    tail = (bracket - head.astype(f32)).astype(bf16)
    return (dot(head, block, dims) + dot(tail, block, dims)).astype(bf16)


def sweeps(where, rhs, wide, inverse, beside):
    share = (CHUNKS, COLS, 128)
    anywhere = pl.BlockSpec(memory_space=pl.ANY)
    return pl.pallas_call(
        sweep_kernel,
        in_specs=[pl.BlockSpec(memory_space=pltpu.SMEM)]
        + [pl.BlockSpec(memory_space=pltpu.VMEM)] * 4
        + [anywhere] * 22,
        out_specs=[pl.BlockSpec(memory_space=pltpu.VMEM)] * 4,
        out_shape=[jax.ShapeDtypeStruct(share, bf16)] * 4,
        scratch_shapes=[
            pltpu.VMEM((SA, 7 * WSN), bf16),
            pltpu.VMEM((SA, WSN), bf16),
            pltpu.VMEM((4 * COLS, SA), bf16),
            pltpu.SemaphoreType.DMA((4,)),
            pltpu.SemaphoreType.DMA((4,)),
            pltpu.SemaphoreType.DMA((4,)),
        ],
        compiler_params=pltpu.CompilerParams(vmem_limit_bytes=48 * MIB),
        name="sweeps",
    )(where, *rhs, *wide, *inverse, *beside)


def extract_kernel(slots, own, near, far, send, table):
    for d, ref in enumerate((own, near, far)):
        for c in range(CHUNKS):
            table[d * CHUNKS + c] = ref[c].astype(f32)
    high = lax.broadcasted_iota(jnp.int32, (COLS, 128), 1) >= BLK

    def for_member(s, carry):
        for i in range(UPD // 128):
            halves = []
            for h in range(2):
                slot = slots[16 * s + 2 * i + h]
                pair = table[slot >> 1]
                halves.append(jnp.where((slot & 1) == h, pair, pltpu.roll(pair, BLK, 1)))
            send[s, :, 128 * i : 128 * i + 128] = jnp.where(high, halves[1], halves[0]).astype(bf16)
        for t in range(4):
            send[s, :, UPD + 128 * t : UPD + 128 * t + 128] = own[4 * s + t]
        return carry

    lax.fori_loop(0, GROUP, for_member, 0)


def extract(slots, own, near, far):
    return pl.pallas_call(
        extract_kernel,
        in_specs=[pl.BlockSpec(memory_space=pltpu.SMEM)] + [pl.BlockSpec(memory_space=pltpu.VMEM)] * 3,
        out_specs=pl.BlockSpec(memory_space=pltpu.VMEM),
        out_shape=jax.ShapeDtypeStruct((GROUP, COLS, SEND), bf16),
        scratch_shapes=[pltpu.VMEM((SPAN * CHUNKS, COLS, 128), f32)],
        compiler_params=pltpu.CompilerParams(vmem_limit_bytes=16 * MIB),
        name="extract_pieces",
    )(slots, own, near, far)


def leaf_backward_kernel(y, pieces, inverse, panel, rows, leaf_x, sep_x):
    inner = (y[0].astype(f32) - dot(pieces[...], panel[0], NN)).astype(bf16)
    leaf_x[0] = dot(inner, inverse[0], NN).astype(bf16).T

    @pl.when(pl.program_id(0) == 0)
    def _():
        sep_x[...] = rows[...].T


def leaf_backward(y, received, inverse, panels):
    return pl.pallas_call(
        leaf_backward_kernel,
        grid=(SN_DEV,),
        in_specs=[
            pl.BlockSpec((1, R, W), lambda j: (j, 0, 0)),
            pl.BlockSpec((R, KB * BLK), lambda j: (0, j)),
            pl.BlockSpec((1, W, W), lambda j: (j, 0, 0)),
            pl.BlockSpec((1, KB * BLK, W), lambda j: (j, 0, 0)),
            pl.BlockSpec((R, WSN), lambda j: (0, UPD // WSN)),
        ],
        out_specs=[
            pl.BlockSpec((1, W, R), lambda j: (j, 0, 0)),
            pl.BlockSpec((WSN, R), lambda j: (0, 0)),
        ],
        out_shape=[
            jax.ShapeDtypeStruct((SN_DEV, W, R), bf16),
            jax.ShapeDtypeStruct((WSN, R), bf16),
        ],
        compiler_params=pltpu.CompilerParams(dimension_semantics=("arbitrary",), vmem_limit_bytes=24 * MIB),
        name="leaf_backward",
    )(y, received, inverse, panels, received)


def along_leaf(block, distance):
    devices = range(lax.axis_size("leaf"))
    route = [(i - distance, i) for i in devices if i - distance in devices]
    return lax.ppermute(block, "leaf", route)


def hop(block, *chips, cores=(0, 1)):
    return lax.ppermute(block, "sub", [(2 * a + c, 2 * b + c) for a, b in chips for c in cores])


def swap(block, cores=(0, 1)):
    return lax.ppermute(block, "sub", [(2 * HUB + c, 2 * HUB + 1 - c) for c in cores])


def gather_factor(factor, inverse, chip):
    beside = lax.dynamic_slice(factor, (0, 2 * WSN * chip), (WSN, WSN))
    inv_near = hop(inverse, (0, 3), (1, 0))
    beside_near = hop(beside, (0, 3), (1, 0), cores=(1,))
    inv2 = hop(inverse, (2, 3))
    beside2 = hop(beside, (2, 3), cores=(1,))
    wide1_way = hop(factor[:, : 2 * WSN], (1, 0))
    wide2 = hop(factor[:, : 4 * WSN], (2, 3))
    inv1 = hop(inv_near, (0, 3))
    beside1 = hop(beside_near, (0, 3), cores=(1,))
    wide1 = hop(wide1_way, (0, 3))
    wide3 = factor[:, : 6 * WSN]
    inverses, besides, wides = [], [], []
    for block in (inv_near, inv1, inv2, inverse):
        inverses += [block, swap(block)]
    for block in (beside_near, beside1, beside2, beside):
        besides += [block, swap(block, cores=(1,))]
    for block in (wide1, wide2, wide3):
        wides += [block, swap(block)]
    return wides, inverses, besides


def shards(
    leaf_right,
    leaf_inverse,
    panels,
    leaf_subtree,
    panel_block,
    separator_right,
    separator_inverse,
    separator_factor,
):
    section = lax.axis_index("leaf")
    member = lax.axis_index("sub")
    chip, core = member // 2, member % 2
    row_blocks = SA // BLK
    own_slots = ((section - leaf_subtree)[:, None] * row_blocks + panel_block).reshape(-1)
    slots = lax.all_gather(own_slots, "sub", axis=0, tiled=True)
    wides, inverses, besides = gather_factor(separator_factor, separator_inverse, chip)
    y, send = leaf_forward(leaf_right, leaf_inverse, panels, separator_right)
    received = lax.all_to_all(send.reshape(GROUP, COLS, SEND), "sub", 0, 0, tiled=True)
    base, near, far = scatter(slots, received)
    near_sum = along_leaf(near, -1).astype(f32)
    far_sum = along_leaf(far, -2).astype(f32)
    rhs = (base - near_sum - far_sum).astype(bf16)
    to_hub = [hop(rhs, (k, HUB)) for k in range(3)] + [rhs]
    where = jnp.stack([chip, core]).astype(jnp.int32)
    shares = sweeps(where, to_hub, wides, inverses, besides)
    own = shares[3]
    back = [hop(shares[k], (HUB, k)) for k in range(3)]
    own = jnp.where(chip == 3, own, jnp.where(chip == 2, back[2], jnp.where(chip == 1, back[1], back[0])))
    pieces = extract(slots, own, along_leaf(own, 1), along_leaf(own, 2))
    pieces = lax.all_to_all(pieces, "sub", 0, 0, tiled=True).reshape(R, SEND)
    return tuple(leaf_backward(y, pieces, leaf_inverse, panels))


def solution(mesh):
    placed = (
        P(("leaf", "sub"), None, None),
        P(("leaf", "sub"), None, None),
        P(("leaf", "sub"), None, None),
        P(("leaf", "sub")),
        P(("leaf", "sub"), None),
        P(("leaf", "sub"), None),
        P(("leaf", "sub"), None),
        P(("leaf", "sub"), None),
    )
    return jax.shard_map(
        shards,
        mesh=mesh,
        in_specs=placed,
        out_specs=(P(("leaf", "sub"), None, None), P(("leaf", "sub"), None)),
        check_vma=False,
    )
```

```python
import jax
import jax.numpy as jnp
from jax import lax
from jax.experimental import pallas as pl
from jax.experimental.pallas import tpu as pltpu
from jax.sharding import PartitionSpec as P

W = 512
WSN = 512
SA = 4096
R = 256
BLK = 64
KB = 4
SPAN = 3
SN_DEV = 4
GROUP = 8
COLS = R // GROUP
CHUNKS = SA // 128
UPD = SN_DEV * KB * BLK
SLOT = UPD + WSN
SEND = SLOT + 128
HUB = 3
bf16 = jnp.bfloat16
f32 = jnp.float32
NT = (((1,), (1,)), ((), ()))
NN = (((1,), (0,)), ((), ()))
MIB = 1 << 20
WHOLE = 60 * MIB


def dot(a, b, dims):
    return lax.dot_general(a, b, dims, preferred_element_type=f32)


def for_each_source(where, visit):
    for chip, wide in ((2, 4 * WSN), (1, 2 * WSN), (0, WSN)):

        @pl.when(where[0] == chip)
        def _():
            visit(chip, wide)


def leaf_forward_kernel(
    where, slots, right, inverse, panel, sep_right, half, factor, sep_inverse, y_out, send, pack2, pack1, pack0, sems
):
    j = pl.program_id(0)
    packs = (pack0, pack1, pack2)

    def begin(chip, wide):
        rows = sep_inverse if chip == 0 else factor.at[:, 0:wide]
        pltpu.make_async_copy(rows, packs[chip].at[:, 0:wide], sems.at[0]).start()
        rest = packs[chip].at[:, wide : wide + WSN // 2]

        @pl.when(where[1] == 1)
        def _():
            beside = factor.at[:, 2 * WSN * chip : 2 * WSN * chip + WSN // 2]
            pltpu.make_async_copy(beside, rest, sems.at[1]).start()

        @pl.when(where[1] == 0)
        def _():
            pltpu.make_async_copy(half, rest, sems.at[1]).start()

    def end(chip, wide):
        whole, rest = packs[chip].at[:, 0:wide], packs[chip].at[:, wide : wide + WSN // 2]
        pltpu.make_async_copy(whole, whole, sems.at[0]).wait()
        pltpu.make_async_copy(rest, rest, sems.at[1]).wait()

    @pl.when(j == 0)
    def _():
        for_each_source(where, begin)
        send[:, UPD:SLOT] = sep_right[...].T
        send[:, SLOT:] = jnp.broadcast_to(slots[...], (R, 128)).astype(bf16)

    y = dot(right[0].T, inverse[0], NT).astype(bf16)
    y_out[0] = y
    send[:, pl.ds(pl.multiple_of(j * KB * BLK, 128), KB * BLK)] = dot(y, panel[0], NT).astype(bf16)

    @pl.when(j == SN_DEV - 1)
    def _():
        for_each_source(where, end)


def leaf_forward(where, slots, right, inverse, panels, sep_right, half, factor, sep_inverse):
    hbm = pl.BlockSpec(memory_space=pltpu.HBM)
    sizes = [(WSN, n * WSN + WSN // 2) for n in (4, 2, 1)]
    return pl.pallas_call(
        leaf_forward_kernel,
        grid=(SN_DEV,),
        in_specs=[
            pl.BlockSpec(memory_space=pltpu.SMEM),
            pl.BlockSpec((1, 128), lambda j: (0, 0)),
            pl.BlockSpec((1, W, R), lambda j: (j, 0, 0)),
            pl.BlockSpec((1, W, W), lambda j: (j, 0, 0)),
            pl.BlockSpec((1, KB * BLK, W), lambda j: (j, 0, 0)),
            pl.BlockSpec((WSN, R), lambda j: (0, 0)),
            hbm,
            hbm,
            hbm,
        ],
        out_specs=[
            pl.BlockSpec((1, R, W), lambda j: (j, 0, 0)),
            pl.BlockSpec((R, SEND), lambda j: (0, 0)),
        ]
        + [pl.BlockSpec(size, lambda j: (0, 0)) for size in sizes],
        out_shape=[
            jax.ShapeDtypeStruct((SN_DEV, R, W), bf16),
            jax.ShapeDtypeStruct((R, SEND), bf16),
        ]
        + [jax.ShapeDtypeStruct(size, bf16) for size in sizes],
        scratch_shapes=[pltpu.SemaphoreType.DMA((2,))],
        compiler_params=pltpu.CompilerParams(dimension_semantics=("arbitrary",), vmem_limit_bytes=WHOLE),
        name="leaf_forward",
    )(where, slots, right, inverse, panels, sep_right, half, factor, sep_inverse)


def scatter_kernel(received, base, near, far, slots_out, table, slots, sem):
    slots_out[...] = received[:, 0, SLOT:].astype(f32).astype(jnp.int32)
    to_scalars = pltpu.make_async_copy(slots_out, slots, sem)
    to_scalars.start()
    table[...] = jnp.zeros_like(table)
    high = lax.broadcasted_iota(jnp.int32, (COLS, 128), 1) >= BLK
    to_scalars.wait()

    def from_member(s, carry):
        for i in range(UPD // 128):
            pair = received[s, :, 128 * i : 128 * i + 128].astype(f32)
            turned = pltpu.roll(pair, BLK, 1)
            for h in range(2):
                slot = slots[s, 2 * i + h]
                want_high = (slot & 1) == 1
                moved = jnp.where(want_high, turned if h == 0 else pair, pair if h == 0 else turned)
                row = slot >> 1
                table[row] = table[row] + jnp.where(high == want_high, moved, 0.0)
        return carry

    lax.fori_loop(0, GROUP, from_member, 0)
    for c in range(CHUNKS):
        first = UPD + 128 * (c % 4)
        base[c] = received[c // 4, :, first : first + 128].astype(f32) - table[c]
        near[c] = table[CHUNKS + c].astype(bf16)
        far[c] = table[2 * CHUNKS + c].astype(bf16)


def scatter(received):
    share = (CHUNKS, COLS, 128)
    return pl.pallas_call(
        scatter_kernel,
        in_specs=[pl.BlockSpec(memory_space=pltpu.VMEM)],
        out_specs=[pl.BlockSpec(memory_space=pltpu.VMEM)] * 4,
        out_shape=[
            jax.ShapeDtypeStruct(share, f32),
            jax.ShapeDtypeStruct(share, bf16),
            jax.ShapeDtypeStruct(share, bf16),
            jax.ShapeDtypeStruct((GROUP, 128), jnp.int32),
        ],
        scratch_shapes=[
            pltpu.VMEM((SPAN * CHUNKS, COLS, 128), f32),
            pltpu.SMEM((GROUP, 128), jnp.int32),
            pltpu.SemaphoreType.DMA(()),
        ],
        compiler_params=pltpu.CompilerParams(vmem_limit_bytes=16 * MIB),
        name="scatter_updates",
    )(received)


def load_rows(core, k, blocks, lower, diagonal, sems):
    odd = slice((2 * k + 1) * WSN, (2 * k + 2) * WSN)
    width = 2 * k * WSN
    for other in (0, 1):
        q = 2 * k + (1 - core if other else core)
        rows = pl.ds(pl.multiple_of(q * WSN, WSN), WSN)
        wide, inverse = blocks[k][other]
        block = wide.at[:, 0:WSN] if k == 0 else inverse
        pltpu.make_async_copy(block, diagonal.at[rows], sems.at[0, k]).start()
        if k > 0:
            pltpu.make_async_copy(wide.at[:, 0:width], lower.at[rows, 0:width], sems.at[1, k]).start()
        for c in (0, 1):
            sender = 1 - c if other else c

            @pl.when(core == c)
            def _():
                if k == HUB:
                    if sender == 1:
                        block = wide.at[:, width : width + WSN]
                        dst = lower.at[odd, width : width + WSN]
                        pltpu.make_async_copy(block, dst, sems.at[2, k]).start()
                else:
                    first = WSN if k == 0 else width
                    block = wide.at[:, first : first + WSN // 2]
                    at = width + (1 - sender) * (WSN // 2)
                    dst = lower.at[odd, at : at + WSN // 2]
                    pltpu.make_async_copy(block, dst, sems.at[2, k]).start()


def await_rows(k, lower, diagonal, sems):
    pair = slice(2 * k * WSN, (2 * k + 2) * WSN)
    both = diagonal.at[pair]
    pltpu.make_async_copy(both, both, sems.at[0, k]).wait()
    if k > 0:
        slab = lower.at[pair, 0 : 2 * k * WSN]
        pltpu.make_async_copy(slab, slab, sems.at[1, k]).wait()
    single = lower.at[(2 * k + 1) * WSN : (2 * k + 2) * WSN, 2 * k * WSN : (2 * k + 1) * WSN]
    pltpu.make_async_copy(single, single, sems.at[2, k]).wait()


def forward_row(q, state, lower, diagonal):
    here = slice(q * WSN, (q + 1) * WSN)
    bracket = state[:, here].astype(f32)
    if q > 0:
        bracket = bracket - dot(state[:, : q * WSN], lower[here, : q * WSN], NT)
    state[:, here] = by_inverse(bracket, diagonal[here], NT)


def head_kernel(where, *refs):
    rhs = refs[0:4]
    blocks = {0: ((refs[4], None), (refs[5], None)), 1: ((refs[6], refs[8]), (refs[7], refs[9]))}
    state, lower, diagonal, shares, rhs_sem, sems = refs[10:]

    @pl.when(where[0] == HUB)
    def _():
        for k in range(4):
            pltpu.make_async_copy(rhs[k], shares.at[k], rhs_sem.at[k]).start()
        for k in (0, 1):
            load_rows(where[1], k, blocks, lower, diagonal, sems)
        for k in range(4):
            pltpu.make_async_copy(rhs[k], shares.at[k], rhs_sem.at[k]).wait()
            for c in range(CHUNKS):
                state[COLS * k : COLS * k + COLS, 128 * c : 128 * c + 128] = shares[k, c]
        for k in (0, 1):
            await_rows(k, lower, diagonal, sems)
            for q in (2 * k, 2 * k + 1):
                forward_row(q, state, lower, diagonal)


def rest_kernel(where, *refs):
    begun = refs[0]
    blocks = {
        0: ((refs[1], None), (refs[2], None)),
        1: ((refs[3], refs[5]), (refs[4], refs[6])),
        2: ((refs[7], refs[9]), (refs[8], refs[10])),
        3: ((refs[11], refs[13]), (refs[12], refs[14])),
    }
    outs = refs[15:19]
    lower, diagonal, state, state_sem, sems = refs[19:]

    @pl.when(where[0] == HUB)
    def _():
        pltpu.make_async_copy(begun, state, state_sem).start()
        for k in (2, 3, 1, 0):
            load_rows(where[1], k, blocks, lower, diagonal, sems)
        pltpu.make_async_copy(begun, state, state_sem).wait()
        for k in (2, 3):
            await_rows(k, lower, diagonal, sems)
            for q in (2 * k, 2 * k + 1):
                forward_row(q, state, lower, diagonal)
        for q in reversed(range(8)):
            if q in (1, 3):
                await_rows(q // 2, lower, diagonal, sems)
            here = slice(q * WSN, (q + 1) * WSN)
            bracket = state[:, here].astype(f32)
            if q < 7:
                bracket = bracket - dot(state[:, (q + 1) * WSN :], lower[(q + 1) * WSN :, here], NN)
            solved = by_inverse(bracket, diagonal[here], NN)
            state[:, here] = solved
            for k in range(4):
                for t in range(4):
                    outs[k][4 * q + t] = solved[COLS * k : COLS * k + COLS, 128 * t : 128 * t + 128]


def by_inverse(bracket, block, dims):
    head = bracket.astype(bf16)
    tail = (bracket - head.astype(f32)).astype(bf16)
    return (dot(head, block, dims) + dot(tail, block, dims)).astype(bf16)


def sweep_head(where, *blocks):
    share = (CHUNKS, COLS, 128)
    hbm = pl.BlockSpec(memory_space=pltpu.HBM)
    return pl.pallas_call(
        head_kernel,
        in_specs=[pl.BlockSpec(memory_space=pltpu.SMEM)] + [hbm] * len(blocks),
        out_specs=pl.BlockSpec(memory_space=pltpu.VMEM),
        out_shape=jax.ShapeDtypeStruct((4 * COLS, SA), bf16),
        scratch_shapes=[
            pltpu.VMEM((4 * WSN, 3 * WSN), bf16),
            pltpu.VMEM((4 * WSN, WSN), bf16),
            pltpu.VMEM((4, *share), bf16),
            pltpu.SemaphoreType.DMA((4,)),
            pltpu.SemaphoreType.DMA((3, 2)),
        ],
        compiler_params=pltpu.CompilerParams(vmem_limit_bytes=20 * MIB),
        name="sweep_head",
    )(where, *blocks)


def sweep_rest(where, *blocks):
    share = (CHUNKS, COLS, 128)
    hbm = pl.BlockSpec(memory_space=pltpu.HBM)
    return pl.pallas_call(
        rest_kernel,
        in_specs=[pl.BlockSpec(memory_space=pltpu.SMEM)] + [hbm] * len(blocks),
        out_specs=[pl.BlockSpec(memory_space=pltpu.VMEM)] * 4,
        out_shape=[jax.ShapeDtypeStruct(share, bf16)] * 4,
        scratch_shapes=[
            pltpu.VMEM((SA, 7 * WSN), bf16),
            pltpu.VMEM((SA, WSN), bf16),
            pltpu.VMEM((4 * COLS, SA), bf16),
            pltpu.SemaphoreType.DMA(()),
            pltpu.SemaphoreType.DMA((3, 4)),
        ],
        compiler_params=pltpu.CompilerParams(vmem_limit_bytes=42 * MIB),
        name="sweep_rest",
    )(where, *blocks)


def extract_kernel(slots, own, near, far, send, table):
    for d, ref in enumerate((own, near, far)):
        for c in range(CHUNKS):
            table[d * CHUNKS + c] = ref[c].astype(f32)
    high = lax.broadcasted_iota(jnp.int32, (COLS, 128), 1) >= BLK

    def for_member(s, carry):
        for i in range(UPD // 128):
            halves = []
            for h in range(2):
                slot = slots[s, 2 * i + h]
                pair = table[slot >> 1]
                halves.append(jnp.where((slot & 1) == h, pair, pltpu.roll(pair, BLK, 1)))
            send[s, :, 128 * i : 128 * i + 128] = jnp.where(high, halves[1], halves[0]).astype(bf16)
        return carry

    lax.fori_loop(0, GROUP, for_member, 0)


def extract(slots, own, near, far):
    return pl.pallas_call(
        extract_kernel,
        in_specs=[pl.BlockSpec(memory_space=pltpu.SMEM)] + [pl.BlockSpec(memory_space=pltpu.VMEM)] * 3,
        out_specs=pl.BlockSpec(memory_space=pltpu.VMEM),
        out_shape=jax.ShapeDtypeStruct((GROUP, COLS, UPD), bf16),
        scratch_shapes=[pltpu.VMEM((SPAN * CHUNKS, COLS, 128), f32)],
        compiler_params=pltpu.CompilerParams(vmem_limit_bytes=16 * MIB),
        name="extract_pieces",
    )(slots, own, near, far)


def leaf_backward_kernel(y, pieces, inverse, panel, rows, leaf_x, sep_x):
    inner = (y[0].astype(f32) - dot(pieces[...], panel[0], NN)).astype(bf16)
    leaf_x[0] = dot(inner, inverse[0], NN).astype(bf16).T

    @pl.when(pl.program_id(0) == 0)
    def _():
        for m in range(GROUP):
            for t in range(WSN // 128):
                sep_x[128 * t : 128 * t + 128, COLS * m : COLS * m + COLS] = rows[m, t].T


def leaf_backward(y, pieces, inverse, panels, rows):
    return pl.pallas_call(
        leaf_backward_kernel,
        grid=(SN_DEV,),
        in_specs=[
            pl.BlockSpec((1, R, W), lambda j: (j, 0, 0)),
            pl.BlockSpec((R, KB * BLK), lambda j: (0, j)),
            pl.BlockSpec((1, W, W), lambda j: (j, 0, 0)),
            pl.BlockSpec((1, KB * BLK, W), lambda j: (j, 0, 0)),
            pl.BlockSpec((GROUP, WSN // 128, COLS, 128), lambda j: (0, 0, 0, 0)),
        ],
        out_specs=[
            pl.BlockSpec((1, W, R), lambda j: (j, 0, 0)),
            pl.BlockSpec((WSN, R), lambda j: (0, 0)),
        ],
        out_shape=[
            jax.ShapeDtypeStruct((SN_DEV, W, R), bf16),
            jax.ShapeDtypeStruct((WSN, R), bf16),
        ],
        compiler_params=pltpu.CompilerParams(dimension_semantics=("arbitrary",), vmem_limit_bytes=WHOLE),
        name="leaf_backward",
    )(y, pieces, inverse, panels, rows)


def along_leaf(block, distance):
    devices = range(lax.axis_size("leaf"))
    route = [(i - distance, i) for i in devices if i - distance in devices]
    return lax.ppermute(block, "leaf", route)


def hop(block, *chips, cores=(0, 1)):
    return lax.ppermute(block, "sub", [(2 * a + c, 2 * b + c) for a, b in chips for c in cores])


def swap(block, cores=(0, 1)):
    return lax.ppermute(block, "sub", [(2 * HUB + c, 2 * HUB + 1 - c) for c in cores])


def shards(
    leaf_right,
    leaf_inverse,
    panels,
    leaf_subtree,
    panel_block,
    separator_right,
    separator_inverse,
    separator_factor,
):
    section = lax.axis_index("leaf")
    member = lax.axis_index("sub")
    chip, core = member // 2, member % 2
    where = jnp.stack([chip, core]).astype(jnp.int32)
    row_blocks = SA // BLK
    own_slots = ((section - leaf_subtree)[:, None] * row_blocks + panel_block).reshape(1, -1)
    own_slots = jnp.pad(own_slots.astype(f32), ((0, 0), (0, 128 - SN_DEV * KB)))
    inverse2, inverse1 = hop(separator_inverse, (2, HUB)), hop(separator_inverse, (1, HUB))
    factors = (separator_factor, swap(separator_factor))
    inverses = (separator_inverse, swap(separator_inverse))
    half = lax.dynamic_slice(separator_factor, (0, 2 * WSN * chip + WSN // 2), (WSN, WSN // 2))
    half = lax.ppermute(half, "sub", [(2 * k + 1, 2 * k) for k in range(3)])
    y, send, *packs = leaf_forward(
        where, own_slots, leaf_right, leaf_inverse, panels, separator_right, half, separator_factor, separator_inverse
    )
    received = lax.all_to_all(send.reshape(GROUP, COLS, SEND), "sub", 0, 0, tiled=True)
    inverse1, inverse2 = (inverse1, swap(inverse1)), (inverse2, swap(inverse2))
    received, packs, factors, inverses, inverse1, inverse2 = lax.optimization_barrier(
        (received, packs, factors, inverses, inverse1, inverse2)
    )
    pack2, pack1, pack0 = (hop(block, (k, HUB)) for block, k in zip(packs, (2, 1, 0)))
    base, near, far, slots = scatter(received)
    near_sum = along_leaf(near, -1).astype(f32)
    far_sum = along_leaf(far, -2).astype(f32)
    rhs = (base - near_sum - far_sum).astype(bf16)
    to_hub = [None, hop(rhs, (1, HUB)), hop(rhs, (2, HUB)), rhs]
    rhs, pack0 = lax.optimization_barrier((rhs, pack0))
    to_hub[0] = hop(rhs, (0, HUB))
    pack0, pack1 = lax.optimization_barrier((pack0, pack1, to_hub[0]))[:2]
    pack0, pack1 = (pack0, swap(pack0)), (pack1, swap(pack1))
    pack2 = lax.optimization_barrier((pack2, *to_hub[:3], pack0, pack1))[0]
    pack2 = (pack2, swap(pack2))
    begun = sweep_head(where, *to_hub, *pack0, *pack1, *inverse1)
    shares = sweep_rest(where, begun, *pack0, *pack1, *inverse1, *pack2, *inverse2, *factors, *inverses)
    back = [hop(shares[k], (HUB, k)) for k in range(3)] + [shares[HUB]]
    own = jnp.where(chip == 3, back[3], jnp.where(chip == 2, back[2], jnp.where(chip == 1, back[1], back[0])))
    pieces = extract(slots, own, along_leaf(own, 1), along_leaf(own, 2))
    rows = lax.all_to_all(own.reshape(GROUP, WSN // 128, COLS, 128), "sub", 0, 0, tiled=True)
    pieces = lax.all_to_all(pieces, "sub", 0, 0, tiled=True).reshape(R, UPD)
    return tuple(leaf_backward(y, pieces, leaf_inverse, panels, rows))


def solution(mesh):
    placed = (
        P(("leaf", "sub"), None, None),
        P(("leaf", "sub"), None, None),
        P(("leaf", "sub"), None, None),
        P(("leaf", "sub")),
        P(("leaf", "sub"), None),
        P(("leaf", "sub"), None),
        P(("leaf", "sub"), None),
        P(("leaf", "sub"), None),
    )
    return jax.shard_map(
        shards,
        mesh=mesh,
        in_specs=placed,
        out_specs=(P(("leaf", "sub"), None, None), P(("leaf", "sub"), None)),
        check_vma=False,
    )
```

```python
import jax
import jax.numpy as jnp
from jax import lax
from jax.experimental import pallas as pl
from jax.experimental.pallas import tpu as pltpu
from jax.sharding import PartitionSpec as P

W = 512
WSN = 512
SA = 4096
R = 256
BLK = 64
KB = 4
SPAN = 3
SN_DEV = 4
GROUP = 8
COLS = R // GROUP
CHUNKS = SA // 128
UPD = SN_DEV * KB * BLK
SLOT = UPD + WSN
SEND = SLOT + 128
HUB = 3
bf16 = jnp.bfloat16
f32 = jnp.float32
NT = (((1,), (1,)), ((), ()))
NN = (((1,), (0,)), ((), ()))
MIB = 1 << 20
WHOLE = 60 * MIB


def dot(a, b, dims):
    return lax.dot_general(a, b, dims, preferred_element_type=f32)


def for_each_source(where, visit):
    for chip, wide in ((2, 4 * WSN), (1, 2 * WSN), (0, 0)):

        @pl.when(where[0] == chip)
        def _():
            visit(chip, wide)


def leaf_forward_kernel(
    where, subtree, block, right, inverse, panel, sep_right, half, factor, y_out, send, pack2, pack1, pack0, sems
):
    j = pl.program_id(0)
    packs = (pack0, pack1, pack2)

    def begin(chip, wide):
        if wide:
            pltpu.make_async_copy(factor.at[:, 0:wide], packs[chip].at[:, 0:wide], sems.at[0]).start()
        rest = packs[chip].at[:, wide : wide + WSN // 2]

        @pl.when(where[1] == 1)
        def _():
            beside = factor.at[:, 2 * WSN * chip : 2 * WSN * chip + WSN // 2]
            pltpu.make_async_copy(beside, rest, sems.at[1]).start()

        @pl.when(where[1] == 0)
        def _():
            pltpu.make_async_copy(half, rest, sems.at[1]).start()

    def end(chip, wide):
        if wide:
            whole = packs[chip].at[:, 0:wide]
            pltpu.make_async_copy(whole, whole, sems.at[0]).wait()
        rest = packs[chip].at[:, wide : wide + WSN // 2]
        pltpu.make_async_copy(rest, rest, sems.at[1]).wait()

    @pl.when(j == 0)
    def _():
        for_each_source(where, begin)
        send[:, UPD:SLOT] = sep_right[...].T
        lane = lax.broadcasted_iota(jnp.int32, (R, 128), 1)
        slots = jnp.zeros((R, 128), jnp.int32)
        for leaf in range(SN_DEV):
            for k in range(KB):
                slot = (where[2] - subtree[leaf]) * (SA // BLK) + block[leaf, k]
                slots = jnp.where(lane == leaf * KB + k, slot, slots)
        send[:, SLOT:] = slots.astype(f32).astype(bf16)

    y = dot(right[0].T, inverse[0], NT).astype(bf16)
    y_out[0] = y
    send[:, pl.ds(pl.multiple_of(j * KB * BLK, 128), KB * BLK)] = dot(y, panel[0], NT).astype(bf16)

    @pl.when(j == SN_DEV - 1)
    def _():
        for_each_source(where, end)


def leaf_forward(where, subtree, block, right, inverse, panels, sep_right, half, factor):
    hbm = pl.BlockSpec(memory_space=pltpu.HBM)
    sizes = [(WSN, n * WSN + WSN // 2) for n in (4, 2, 0)]
    return pl.pallas_call(
        leaf_forward_kernel,
        grid=(SN_DEV,),
        in_specs=[
            pl.BlockSpec(memory_space=pltpu.SMEM),
            pl.BlockSpec(memory_space=pltpu.SMEM),
            pl.BlockSpec(memory_space=pltpu.SMEM),
            pl.BlockSpec((1, W, R), lambda j: (j, 0, 0)),
            pl.BlockSpec((1, W, W), lambda j: (j, 0, 0)),
            pl.BlockSpec((1, KB * BLK, W), lambda j: (j, 0, 0)),
            pl.BlockSpec((WSN, R), lambda j: (0, 0)),
            hbm,
            hbm,
        ],
        out_specs=[
            pl.BlockSpec((1, R, W), lambda j: (j, 0, 0)),
            pl.BlockSpec((R, SEND), lambda j: (0, 0)),
        ]
        + [pl.BlockSpec(size, lambda j: (0, 0)) for size in sizes],
        out_shape=[
            jax.ShapeDtypeStruct((SN_DEV, R, W), bf16),
            jax.ShapeDtypeStruct((R, SEND), bf16),
        ]
        + [jax.ShapeDtypeStruct(size, bf16) for size in sizes],
        scratch_shapes=[pltpu.SemaphoreType.DMA((2,))],
        compiler_params=pltpu.CompilerParams(dimension_semantics=("arbitrary",), vmem_limit_bytes=WHOLE),
        name="leaf_forward",
    )(where, subtree, block, right, inverse, panels, sep_right, half, factor)


def scatter_kernel(received, base, near, far, slots_out, table, slots, sem):
    slots_out[...] = received[:, 0, SLOT:].astype(f32).astype(jnp.int32)
    to_scalars = pltpu.make_async_copy(slots_out, slots, sem)
    to_scalars.start()
    table[...] = jnp.zeros_like(table)
    high = lax.broadcasted_iota(jnp.int32, (COLS, 128), 1) >= BLK
    to_scalars.wait()

    def from_member(s, carry):
        for i in range(UPD // 128):
            pair = received[s, :, 128 * i : 128 * i + 128].astype(f32)
            turned = pltpu.roll(pair, BLK, 1)
            for h in range(2):
                slot = slots[s, 2 * i + h]
                want_high = (slot & 1) == 1
                moved = jnp.where(want_high, turned if h == 0 else pair, pair if h == 0 else turned)
                row = slot >> 1
                table[row] = table[row] + jnp.where(high == want_high, moved, 0.0)
        return carry

    lax.fori_loop(0, GROUP, from_member, 0)
    for c in range(CHUNKS):
        first = UPD + 128 * (c % 4)
        base[c] = received[c // 4, :, first : first + 128].astype(f32) - table[c]
        near[c] = table[CHUNKS + c].astype(bf16)
        far[c] = table[2 * CHUNKS + c].astype(bf16)


def scatter(received):
    share = (CHUNKS, COLS, 128)
    return pl.pallas_call(
        scatter_kernel,
        in_specs=[pl.BlockSpec(memory_space=pltpu.VMEM)],
        out_specs=[pl.BlockSpec(memory_space=pltpu.VMEM)] * 4,
        out_shape=[
            jax.ShapeDtypeStruct(share, f32),
            jax.ShapeDtypeStruct(share, bf16),
            jax.ShapeDtypeStruct(share, bf16),
            jax.ShapeDtypeStruct((GROUP, 128), jnp.int32),
        ],
        scratch_shapes=[
            pltpu.VMEM((SPAN * CHUNKS, COLS, 128), f32),
            pltpu.SMEM((GROUP, 128), jnp.int32),
            pltpu.SemaphoreType.DMA(()),
        ],
        compiler_params=pltpu.CompilerParams(vmem_limit_bytes=16 * MIB),
        name="scatter_updates",
    )(received)


def load_rows(core, k, blocks, lower, diagonal, sems):
    odd = slice((2 * k + 1) * WSN, (2 * k + 2) * WSN)
    width = 2 * k * WSN
    for other in (0, 1):
        q = 2 * k + (1 - core if other else core)
        rows = pl.ds(pl.multiple_of(q * WSN, WSN), WSN)
        wide, inverse = blocks[k][other]
        pltpu.make_async_copy(inverse, diagonal.at[rows], sems.at[0, k]).start()
        if k > 0:
            pltpu.make_async_copy(wide.at[:, 0:width], lower.at[rows, 0:width], sems.at[1, k]).start()
        for c in (0, 1):
            sender = 1 - c if other else c

            @pl.when(core == c)
            def _():
                if k == HUB:
                    if sender == 1:
                        block = wide.at[:, width : width + WSN]
                        dst = lower.at[odd, width : width + WSN]
                        pltpu.make_async_copy(block, dst, sems.at[2, k]).start()
                else:
                    first = width
                    block = wide.at[:, first : first + WSN // 2]
                    at = width + (1 - sender) * (WSN // 2)
                    dst = lower.at[odd, at : at + WSN // 2]
                    pltpu.make_async_copy(block, dst, sems.at[2, k]).start()


def await_rows(k, lower, diagonal, sems):
    pair = slice(2 * k * WSN, (2 * k + 2) * WSN)
    both = diagonal.at[pair]
    pltpu.make_async_copy(both, both, sems.at[0, k]).wait()
    if k > 0:
        slab = lower.at[pair, 0 : 2 * k * WSN]
        pltpu.make_async_copy(slab, slab, sems.at[1, k]).wait()
    single = lower.at[(2 * k + 1) * WSN : (2 * k + 2) * WSN, 2 * k * WSN : (2 * k + 1) * WSN]
    pltpu.make_async_copy(single, single, sems.at[2, k]).wait()


def forward_row(q, state, lower, diagonal):
    here = slice(q * WSN, (q + 1) * WSN)
    bracket = state[:, here].astype(f32)
    if q > 0:
        bracket = bracket - dot(state[:, : q * WSN], lower[here, : q * WSN], NT)
    state[:, here] = by_inverse(bracket, diagonal[here], NT)


def head_kernel(where, *refs):
    rhs = refs[0:4]
    blocks = {0: ((refs[4], refs[6]), (refs[5], refs[7])), 1: ((refs[8], refs[10]), (refs[9], refs[11]))}
    state, lower, diagonal, shares, rhs_sem, sems = refs[12:]

    @pl.when(where[0] == HUB)
    def _():
        for k in range(4):
            pltpu.make_async_copy(rhs[k], shares.at[k], rhs_sem.at[k]).start()
        for k in (0, 1):
            load_rows(where[1], k, blocks, lower, diagonal, sems)
        for k in range(4):
            pltpu.make_async_copy(rhs[k], shares.at[k], rhs_sem.at[k]).wait()
            for c in range(CHUNKS):
                state[COLS * k : COLS * k + COLS, 128 * c : 128 * c + 128] = shares[k, c]
        for k in (0, 1):
            await_rows(k, lower, diagonal, sems)
            for q in (2 * k, 2 * k + 1):
                forward_row(q, state, lower, diagonal)


def rest_kernel(where, *refs):
    begun = refs[0]
    blocks = {
        0: ((refs[1], refs[3]), (refs[2], refs[4])),
        1: ((refs[5], refs[7]), (refs[6], refs[8])),
        2: ((refs[9], refs[11]), (refs[10], refs[12])),
        3: ((refs[13], refs[15]), (refs[14], refs[16])),
    }
    outs = refs[17:21]
    lower, diagonal, state, state_sem, sems = refs[21:]

    @pl.when(where[0] == HUB)
    def _():
        pltpu.make_async_copy(begun, state, state_sem).start()
        for k in (2, 3, 1, 0):
            load_rows(where[1], k, blocks, lower, diagonal, sems)
        pltpu.make_async_copy(begun, state, state_sem).wait()
        for k in (2, 3):
            await_rows(k, lower, diagonal, sems)
            for q in (2 * k, 2 * k + 1):
                forward_row(q, state, lower, diagonal)
        for q in reversed(range(8)):
            if q in (1, 3):
                await_rows(q // 2, lower, diagonal, sems)
            here = slice(q * WSN, (q + 1) * WSN)
            bracket = state[:, here].astype(f32)
            if q < 7:
                bracket = bracket - dot(state[:, (q + 1) * WSN :], lower[(q + 1) * WSN :, here], NN)
            solved = by_inverse(bracket, diagonal[here], NN)
            state[:, here] = solved
            for k in range(4):
                for t in range(4):
                    outs[k][4 * q + t] = solved[COLS * k : COLS * k + COLS, 128 * t : 128 * t + 128]


def by_inverse(bracket, block, dims):
    head = bracket.astype(bf16)
    tail = (bracket - head.astype(f32)).astype(bf16)
    return (dot(head, block, dims) + dot(tail, block, dims)).astype(bf16)


def sweep_head(where, *blocks):
    share = (CHUNKS, COLS, 128)
    hbm = pl.BlockSpec(memory_space=pltpu.HBM)
    return pl.pallas_call(
        head_kernel,
        in_specs=[pl.BlockSpec(memory_space=pltpu.SMEM)] + [hbm] * len(blocks),
        out_specs=pl.BlockSpec(memory_space=pltpu.VMEM),
        out_shape=jax.ShapeDtypeStruct((4 * COLS, SA), bf16),
        scratch_shapes=[
            pltpu.VMEM((4 * WSN, 3 * WSN), bf16),
            pltpu.VMEM((4 * WSN, WSN), bf16),
            pltpu.VMEM((4, *share), bf16),
            pltpu.SemaphoreType.DMA((4,)),
            pltpu.SemaphoreType.DMA((3, 2)),
        ],
        compiler_params=pltpu.CompilerParams(vmem_limit_bytes=20 * MIB),
        name="sweep_head",
    )(where, *blocks)


def sweep_rest(where, *blocks):
    share = (CHUNKS, COLS, 128)
    hbm = pl.BlockSpec(memory_space=pltpu.HBM)
    return pl.pallas_call(
        rest_kernel,
        in_specs=[pl.BlockSpec(memory_space=pltpu.SMEM)] + [hbm] * len(blocks),
        out_specs=[pl.BlockSpec(memory_space=pltpu.VMEM)] * 4,
        out_shape=[jax.ShapeDtypeStruct(share, bf16)] * 4,
        scratch_shapes=[
            pltpu.VMEM((SA, 7 * WSN), bf16),
            pltpu.VMEM((SA, WSN), bf16),
            pltpu.VMEM((4 * COLS, SA), bf16),
            pltpu.SemaphoreType.DMA(()),
            pltpu.SemaphoreType.DMA((3, 4)),
        ],
        compiler_params=pltpu.CompilerParams(vmem_limit_bytes=42 * MIB),
        name="sweep_rest",
    )(where, *blocks)


def extract_kernel(slots, own, near, far, send, table):
    for d, ref in enumerate((own, near, far)):
        for c in range(CHUNKS):
            table[d * CHUNKS + c] = ref[c].astype(f32)
    high = lax.broadcasted_iota(jnp.int32, (COLS, 128), 1) >= BLK

    def for_member(s, carry):
        for i in range(UPD // 128):
            halves = []
            for h in range(2):
                slot = slots[s, 2 * i + h]
                pair = table[slot >> 1]
                halves.append(jnp.where((slot & 1) == h, pair, pltpu.roll(pair, BLK, 1)))
            send[s, :, 128 * i : 128 * i + 128] = jnp.where(high, halves[1], halves[0]).astype(bf16)
        return carry

    lax.fori_loop(0, GROUP, for_member, 0)


def extract(slots, own, near, far):
    return pl.pallas_call(
        extract_kernel,
        in_specs=[pl.BlockSpec(memory_space=pltpu.SMEM)] + [pl.BlockSpec(memory_space=pltpu.VMEM)] * 3,
        out_specs=pl.BlockSpec(memory_space=pltpu.VMEM),
        out_shape=jax.ShapeDtypeStruct((GROUP, COLS, UPD), bf16),
        scratch_shapes=[pltpu.VMEM((SPAN * CHUNKS, COLS, 128), f32)],
        compiler_params=pltpu.CompilerParams(vmem_limit_bytes=16 * MIB),
        name="extract_pieces",
    )(slots, own, near, far)


def leaf_backward_kernel(y, pieces, inverse, panel, rows, leaf_x, sep_x):
    inner = (y[0].astype(f32) - dot(pieces[...], panel[0], NN)).astype(bf16)
    leaf_x[0] = dot(inner, inverse[0], NN).astype(bf16).T

    @pl.when(pl.program_id(0) == 0)
    def _():
        for m in range(GROUP):
            for t in range(WSN // 128):
                sep_x[128 * t : 128 * t + 128, COLS * m : COLS * m + COLS] = rows[m, t].T


def leaf_backward(y, pieces, inverse, panels, rows):
    return pl.pallas_call(
        leaf_backward_kernel,
        grid=(SN_DEV,),
        in_specs=[
            pl.BlockSpec((1, R, W), lambda j: (j, 0, 0)),
            pl.BlockSpec((R, KB * BLK), lambda j: (0, j)),
            pl.BlockSpec((1, W, W), lambda j: (j, 0, 0)),
            pl.BlockSpec((1, KB * BLK, W), lambda j: (j, 0, 0)),
            pl.BlockSpec((GROUP, WSN // 128, COLS, 128), lambda j: (0, 0, 0, 0)),
        ],
        out_specs=[
            pl.BlockSpec((1, W, R), lambda j: (j, 0, 0)),
            pl.BlockSpec((WSN, R), lambda j: (0, 0)),
        ],
        out_shape=[
            jax.ShapeDtypeStruct((SN_DEV, W, R), bf16),
            jax.ShapeDtypeStruct((WSN, R), bf16),
        ],
        compiler_params=pltpu.CompilerParams(dimension_semantics=("arbitrary",), vmem_limit_bytes=24 * MIB),
        name="leaf_backward",
    )(y, pieces, inverse, panels, rows)


def along_leaf(block, distance):
    devices = range(lax.axis_size("leaf"))
    route = [(i - distance, i) for i in devices if i - distance in devices]
    return lax.ppermute(block, "leaf", route)


def hop(block, *chips, cores=(0, 1)):
    return lax.ppermute(block, "sub", [(2 * a + c, 2 * b + c) for a, b in chips for c in cores])


def swap(block, cores=(0, 1)):
    return lax.ppermute(block, "sub", [(2 * HUB + c, 2 * HUB + 1 - c) for c in cores])


def shards(
    leaf_right,
    leaf_inverse,
    panels,
    leaf_subtree,
    panel_block,
    separator_right,
    separator_inverse,
    separator_factor,
):
    section = lax.axis_index("leaf")
    member = lax.axis_index("sub")
    chip, core = member // 2, member % 2
    where = jnp.stack([chip, core, section]).astype(jnp.int32)
    early = [hop(separator_inverse, (k, HUB)) for k in range(3)]
    factors = (separator_factor, swap(separator_factor))
    inverses = (separator_inverse, swap(separator_inverse))
    half = lax.dynamic_slice(separator_factor, (0, 2 * WSN * chip + WSN // 2), (WSN, WSN // 2))
    half = lax.ppermute(half, "sub", [(2 * k + 1, 2 * k) for k in range(3)])
    y, send, *packs = leaf_forward(
        where,
        leaf_subtree,
        panel_block,
        leaf_right,
        leaf_inverse,
        panels,
        separator_right,
        half,
        separator_factor,
    )
    received = lax.all_to_all(send.reshape(GROUP, COLS, SEND), "sub", 0, 0, tiled=True)
    early = [(block, swap(block)) for block in early]
    received, packs, factors, inverses, early = lax.optimization_barrier(
        (received, packs, factors, inverses, early)
    )
    pack2, pack1, pack0 = (hop(block, (k, HUB)) for block, k in zip(packs, (2, 1, 0)))
    base, near, far, slots = scatter(received)
    near, far = along_leaf(near, -1), along_leaf(far, -2)
    pack1 = lax.optimization_barrier((pack1, near, far))[0]
    pack1 = (pack1, swap(pack1))
    near, far, pack0, pack1 = lax.optimization_barrier((near, far, pack0, pack1))
    rhs = (base - near.astype(f32) - far.astype(f32)).astype(bf16)
    pack0 = (pack0, swap(pack0))
    to_hub = [hop(rhs, (k, HUB)) for k in range(3)] + [rhs]
    pack2 = lax.optimization_barrier((pack2, *to_hub[:3], pack0))[0]
    pack2 = (pack2, swap(pack2))
    begun = sweep_head(where, *to_hub, *pack0, *early[0], *pack1, *early[1])
    shares = sweep_rest(
        where, begun, *pack0, *early[0], *pack1, *early[1], *pack2, *early[2], *factors, *inverses
    )
    back = [hop(shares[k], (HUB, k)) for k in range(3)] + [shares[HUB]]
    own = jnp.where(chip == 3, back[3], jnp.where(chip == 2, back[2], jnp.where(chip == 1, back[1], back[0])))
    pieces = extract(slots, own, along_leaf(own, 1), along_leaf(own, 2))
    rows = lax.all_to_all(own.reshape(GROUP, WSN // 128, COLS, 128), "sub", 0, 0, tiled=True)
    pieces = lax.all_to_all(pieces, "sub", 0, 0, tiled=True).reshape(R, UPD)
    return tuple(leaf_backward(y, pieces, leaf_inverse, panels, rows))


def solution(mesh):
    placed = (
        P(("leaf", "sub"), None, None),
        P(("leaf", "sub"), None, None),
        P(("leaf", "sub"), None, None),
        P(("leaf", "sub")),
        P(("leaf", "sub"), None),
        P(("leaf", "sub"), None),
        P(("leaf", "sub"), None),
        P(("leaf", "sub"), None),
    )
    return jax.shard_map(
        shards,
        mesh=mesh,
        in_specs=placed,
        out_specs=(P(("leaf", "sub"), None, None), P(("leaf", "sub"), None)),
        check_vma=False,
    )
```

```python
import jax
import jax.numpy as jnp
from jax import lax
from jax.experimental import pallas as pl
from jax.experimental.pallas import tpu as pltpu
from jax.sharding import PartitionSpec as P

W = 512
WSN = 512
SA = 4096
R = 256
BLK = 64
KB = 4
SPAN = 3
SN_DEV = 4
GROUP = 8
COLS = R // GROUP
CHUNKS = SA // 128
UPD = SN_DEV * KB * BLK
SLOT = UPD + WSN
SEND = SLOT + 128
HUB = 3
bf16 = jnp.bfloat16
f32 = jnp.float32
NT = (((1,), (1,)), ((), ()))
NN = (((1,), (0,)), ((), ()))
MIB = 1 << 20
WHOLE = 60 * MIB


def dot(a, b, dims):
    return lax.dot_general(a, b, dims, preferred_element_type=f32)


def for_each_source(where, visit):
    for chip, wide in ((2, 4 * WSN), (1, 2 * WSN), (0, 0)):

        @pl.when(where[0] == chip)
        def _():
            visit(chip, wide)


def leaf_forward_kernel(
    where, subtree, block, right, inverse, panel, sep_right, half, factor, y_out, send, pack2, pack1, pack0, sems
):
    j = pl.program_id(0)
    packs = (pack0, pack1, pack2)

    def begin(chip, wide):
        if wide:
            pltpu.make_async_copy(factor.at[:, 0:wide], packs[chip].at[:, 0:wide], sems.at[0]).start()
        rest = packs[chip].at[:, wide : wide + WSN // 2]

        @pl.when(where[1] == 1)
        def _():
            beside = factor.at[:, 2 * WSN * chip : 2 * WSN * chip + WSN // 2]
            pltpu.make_async_copy(beside, rest, sems.at[1]).start()

        @pl.when(where[1] == 0)
        def _():
            pltpu.make_async_copy(half, rest, sems.at[1]).start()

    def end(chip, wide):
        if wide:
            whole = packs[chip].at[:, 0:wide]
            pltpu.make_async_copy(whole, whole, sems.at[0]).wait()
        rest = packs[chip].at[:, wide : wide + WSN // 2]
        pltpu.make_async_copy(rest, rest, sems.at[1]).wait()

    @pl.when(j == 0)
    def _():
        for_each_source(where, begin)
        send[:, UPD:SLOT] = sep_right[...].T
        lane = lax.broadcasted_iota(jnp.int32, (R, 128), 1)
        slots = jnp.zeros((R, 128), jnp.int32)
        for leaf in range(SN_DEV):
            for k in range(KB):
                slot = (where[2] - subtree[leaf]) * (SA // BLK) + block[leaf, k]
                slots = jnp.where(lane == leaf * KB + k, slot, slots)
        send[:, SLOT:] = slots.astype(f32).astype(bf16)

    y = dot(right[0].T, inverse[0], NT).astype(bf16)
    y_out[0] = y
    send[:, pl.ds(pl.multiple_of(j * KB * BLK, 128), KB * BLK)] = dot(y, panel[0], NT).astype(bf16)

    @pl.when(j == SN_DEV - 1)
    def _():
        for_each_source(where, end)


def leaf_forward(where, subtree, block, right, inverse, panels, sep_right, half, factor):
    hbm = pl.BlockSpec(memory_space=pltpu.HBM)
    sizes = [(WSN, n * WSN + WSN // 2) for n in (4, 2, 0)]
    return pl.pallas_call(
        leaf_forward_kernel,
        grid=(SN_DEV,),
        in_specs=[
            pl.BlockSpec(memory_space=pltpu.SMEM),
            pl.BlockSpec(memory_space=pltpu.SMEM),
            pl.BlockSpec(memory_space=pltpu.SMEM),
            pl.BlockSpec((1, W, R), lambda j: (j, 0, 0)),
            pl.BlockSpec((1, W, W), lambda j: (j, 0, 0)),
            pl.BlockSpec((1, KB * BLK, W), lambda j: (j, 0, 0)),
            pl.BlockSpec((WSN, R), lambda j: (0, 0)),
            hbm,
            hbm,
        ],
        out_specs=[
            pl.BlockSpec((1, R, W), lambda j: (j, 0, 0)),
            pl.BlockSpec((R, SEND), lambda j: (0, 0)),
        ]
        + [pl.BlockSpec(size, lambda j: (0, 0)) for size in sizes],
        out_shape=[
            jax.ShapeDtypeStruct((SN_DEV, R, W), bf16),
            jax.ShapeDtypeStruct((R, SEND), bf16),
        ]
        + [jax.ShapeDtypeStruct(size, bf16) for size in sizes],
        scratch_shapes=[pltpu.SemaphoreType.DMA((2,))],
        compiler_params=pltpu.CompilerParams(dimension_semantics=("arbitrary",), vmem_limit_bytes=WHOLE),
        name="leaf_forward",
    )(where, subtree, block, right, inverse, panels, sep_right, half, factor)


def scatter_kernel(received, base, near, far, slots_out, table, slots, sem):
    slots_out[...] = received[:, 0, SLOT:].astype(f32).astype(jnp.int32)
    to_scalars = pltpu.make_async_copy(slots_out, slots, sem)
    to_scalars.start()
    table[...] = jnp.zeros_like(table)
    high = lax.broadcasted_iota(jnp.int32, (COLS, 128), 1) >= BLK
    to_scalars.wait()

    def from_member(s, carry):
        for i in range(UPD // 128):
            pair = received[s, :, 128 * i : 128 * i + 128].astype(f32)
            turned = pltpu.roll(pair, BLK, 1)
            for h in range(2):
                slot = slots[s, 2 * i + h]
                want_high = (slot & 1) == 1
                moved = jnp.where(want_high, turned if h == 0 else pair, pair if h == 0 else turned)
                row = slot >> 1
                table[row] = table[row] + jnp.where(high == want_high, moved, 0.0)
        return carry

    lax.fori_loop(0, GROUP, from_member, 0)
    for c in range(CHUNKS):
        first = UPD + 128 * (c % 4)
        base[c] = received[c // 4, :, first : first + 128].astype(f32) - table[c]
        near[c] = table[CHUNKS + c].astype(bf16)
        far[c] = table[2 * CHUNKS + c].astype(bf16)


def scatter(received):
    share = (CHUNKS, COLS, 128)
    return pl.pallas_call(
        scatter_kernel,
        in_specs=[pl.BlockSpec(memory_space=pltpu.VMEM)],
        out_specs=[pl.BlockSpec(memory_space=pltpu.VMEM)] * 4,
        out_shape=[
            jax.ShapeDtypeStruct(share, f32),
            jax.ShapeDtypeStruct(share, bf16),
            jax.ShapeDtypeStruct(share, bf16),
            jax.ShapeDtypeStruct((GROUP, 128), jnp.int32),
        ],
        scratch_shapes=[
            pltpu.VMEM((SPAN * CHUNKS, COLS, 128), f32),
            pltpu.SMEM((GROUP, 128), jnp.int32),
            pltpu.SemaphoreType.DMA(()),
        ],
        compiler_params=pltpu.CompilerParams(vmem_limit_bytes=16 * MIB),
        name="scatter_updates",
    )(received)


def load_rows(core, k, blocks, lower, diagonal, sems):
    odd = slice((2 * k + 1) * WSN, (2 * k + 2) * WSN)
    width = 2 * k * WSN
    for other in (0, 1):
        q = 2 * k + (1 - core if other else core)
        rows = pl.ds(pl.multiple_of(q * WSN, WSN), WSN)
        wide, inverse = blocks[k][other]
        pltpu.make_async_copy(inverse, diagonal.at[rows], sems.at[0, k]).start()
        if k > 0:
            pltpu.make_async_copy(wide.at[:, 0:width], lower.at[rows, 0:width], sems.at[1, k]).start()
        for c in (0, 1):
            sender = 1 - c if other else c

            @pl.when(core == c)
            def _():
                if k == HUB:
                    if sender == 1:
                        block = wide.at[:, width : width + WSN]
                        dst = lower.at[odd, width : width + WSN]
                        pltpu.make_async_copy(block, dst, sems.at[2, k]).start()
                else:
                    first = width
                    block = wide.at[:, first : first + WSN // 2]
                    at = width + (1 - sender) * (WSN // 2)
                    dst = lower.at[odd, at : at + WSN // 2]
                    pltpu.make_async_copy(block, dst, sems.at[2, k]).start()


def await_rows(k, lower, diagonal, sems):
    pair = slice(2 * k * WSN, (2 * k + 2) * WSN)
    both = diagonal.at[pair]
    pltpu.make_async_copy(both, both, sems.at[0, k]).wait()
    if k > 0:
        slab = lower.at[pair, 0 : 2 * k * WSN]
        pltpu.make_async_copy(slab, slab, sems.at[1, k]).wait()
    single = lower.at[(2 * k + 1) * WSN : (2 * k + 2) * WSN, 2 * k * WSN : (2 * k + 1) * WSN]
    pltpu.make_async_copy(single, single, sems.at[2, k]).wait()


def forward_row(q, state, lower, diagonal):
    here = slice(q * WSN, (q + 1) * WSN)
    bracket = state[:, here].astype(f32)
    if q > 0:
        bracket = bracket - dot(state[:, : q * WSN], lower[here, : q * WSN], NT)
    state[:, here] = by_inverse(bracket, diagonal[here], NT)


def head_kernel(where, *refs):
    rhs = refs[0:4]
    blocks = {0: ((refs[4], refs[6]), (refs[5], refs[7])), 1: ((refs[8], refs[10]), (refs[9], refs[11]))}
    state, lower, diagonal, shares, rhs_sem, sems = refs[12:]

    @pl.when(where[0] == HUB)
    def _():
        for k in range(4):
            pltpu.make_async_copy(rhs[k], shares.at[k], rhs_sem.at[k]).start()
        for k in (0, 1):
            load_rows(where[1], k, blocks, lower, diagonal, sems)
        for k in range(4):
            pltpu.make_async_copy(rhs[k], shares.at[k], rhs_sem.at[k]).wait()
            for c in range(CHUNKS):
                state[COLS * k : COLS * k + COLS, 128 * c : 128 * c + 128] = shares[k, c]
        for k in (0, 1):
            await_rows(k, lower, diagonal, sems)
            for q in (2 * k, 2 * k + 1):
                forward_row(q, state, lower, diagonal)


def rest_kernel(where, *refs):
    begun = refs[0]
    blocks = {
        0: ((refs[1], refs[3]), (refs[2], refs[4])),
        1: ((refs[5], refs[7]), (refs[6], refs[8])),
        2: ((refs[9], refs[11]), (refs[10], refs[12])),
        3: ((refs[13], refs[15]), (refs[14], refs[16])),
    }
    outs = refs[17:21]
    lower, diagonal, state, state_sem, sems = refs[21:]

    @pl.when(where[0] == HUB)
    def _():
        pltpu.make_async_copy(begun, state, state_sem).start()
        for k in (2, 3, 1, 0):
            load_rows(where[1], k, blocks, lower, diagonal, sems)
        pltpu.make_async_copy(begun, state, state_sem).wait()
        for k in (2, 3):
            await_rows(k, lower, diagonal, sems)
            for q in (2 * k, 2 * k + 1):
                forward_row(q, state, lower, diagonal)
        for q in reversed(range(8)):
            if q in (1, 3):
                await_rows(q // 2, lower, diagonal, sems)
            here = slice(q * WSN, (q + 1) * WSN)
            bracket = state[:, here].astype(f32)
            if q < 7:
                bracket = bracket - dot(state[:, (q + 1) * WSN :], lower[(q + 1) * WSN :, here], NN)
            solved = by_inverse(bracket, diagonal[here], NN)
            state[:, here] = solved
            for k in range(4):
                for t in range(4):
                    outs[k][4 * q + t] = solved[COLS * k : COLS * k + COLS, 128 * t : 128 * t + 128]


def by_inverse(bracket, block, dims):
    head = bracket.astype(bf16)
    tail = (bracket - head.astype(f32)).astype(bf16)
    both = dot(jnp.concatenate([head, tail], axis=0), block, dims)
    rows = bracket.shape[0]
    return (both[:rows] + both[rows:]).astype(bf16)


def sweep_head(where, *blocks):
    share = (CHUNKS, COLS, 128)
    hbm = pl.BlockSpec(memory_space=pltpu.HBM)
    return pl.pallas_call(
        head_kernel,
        in_specs=[pl.BlockSpec(memory_space=pltpu.SMEM)] + [hbm] * len(blocks),
        out_specs=pl.BlockSpec(memory_space=pltpu.VMEM),
        out_shape=jax.ShapeDtypeStruct((4 * COLS, SA), bf16),
        scratch_shapes=[
            pltpu.VMEM((4 * WSN, 3 * WSN), bf16),
            pltpu.VMEM((4 * WSN, WSN), bf16),
            pltpu.VMEM((4, *share), bf16),
            pltpu.SemaphoreType.DMA((4,)),
            pltpu.SemaphoreType.DMA((3, 2)),
        ],
        compiler_params=pltpu.CompilerParams(vmem_limit_bytes=20 * MIB),
        name="sweep_head",
    )(where, *blocks)


def sweep_rest(where, *blocks):
    share = (CHUNKS, COLS, 128)
    hbm = pl.BlockSpec(memory_space=pltpu.HBM)
    return pl.pallas_call(
        rest_kernel,
        in_specs=[pl.BlockSpec(memory_space=pltpu.SMEM)] + [hbm] * len(blocks),
        out_specs=[pl.BlockSpec(memory_space=pltpu.VMEM)] * 4,
        out_shape=[jax.ShapeDtypeStruct(share, bf16)] * 4,
        scratch_shapes=[
            pltpu.VMEM((SA, 7 * WSN), bf16),
            pltpu.VMEM((SA, WSN), bf16),
            pltpu.VMEM((4 * COLS, SA), bf16),
            pltpu.SemaphoreType.DMA(()),
            pltpu.SemaphoreType.DMA((3, 4)),
        ],
        compiler_params=pltpu.CompilerParams(vmem_limit_bytes=42 * MIB),
        name="sweep_rest",
    )(where, *blocks)


def extract_kernel(slots, own, near, far, send, table):
    for d, ref in enumerate((own, near, far)):
        for c in range(CHUNKS):
            table[d * CHUNKS + c] = ref[c].astype(f32)
    high = lax.broadcasted_iota(jnp.int32, (COLS, 128), 1) >= BLK

    def for_member(s, carry):
        for i in range(UPD // 128):
            halves = []
            for h in range(2):
                slot = slots[s, 2 * i + h]
                pair = table[slot >> 1]
                halves.append(jnp.where((slot & 1) == h, pair, pltpu.roll(pair, BLK, 1)))
            send[s, :, 128 * i : 128 * i + 128] = jnp.where(high, halves[1], halves[0]).astype(bf16)
        return carry

    lax.fori_loop(0, GROUP, for_member, 0)


def extract(slots, own, near, far):
    return pl.pallas_call(
        extract_kernel,
        in_specs=[pl.BlockSpec(memory_space=pltpu.SMEM)] + [pl.BlockSpec(memory_space=pltpu.VMEM)] * 3,
        out_specs=pl.BlockSpec(memory_space=pltpu.VMEM),
        out_shape=jax.ShapeDtypeStruct((GROUP, COLS, UPD), bf16),
        scratch_shapes=[pltpu.VMEM((SPAN * CHUNKS, COLS, 128), f32)],
        compiler_params=pltpu.CompilerParams(vmem_limit_bytes=16 * MIB),
        name="extract_pieces",
    )(slots, own, near, far)


def leaf_backward_kernel(y, pieces, inverse, panel, rows, leaf_x, sep_x):
    inner = (y[0].astype(f32) - dot(pieces[...], panel[0], NN)).astype(bf16)
    leaf_x[0] = dot(inner, inverse[0], NN).astype(bf16).T

    @pl.when(pl.program_id(0) == 0)
    def _():
        for m in range(GROUP):
            for t in range(WSN // 128):
                sep_x[128 * t : 128 * t + 128, COLS * m : COLS * m + COLS] = rows[m, t].T


def leaf_backward(y, pieces, inverse, panels, rows):
    return pl.pallas_call(
        leaf_backward_kernel,
        grid=(SN_DEV,),
        in_specs=[
            pl.BlockSpec((1, R, W), lambda j: (j, 0, 0)),
            pl.BlockSpec((R, KB * BLK), lambda j: (0, j)),
            pl.BlockSpec((1, W, W), lambda j: (j, 0, 0)),
            pl.BlockSpec((1, KB * BLK, W), lambda j: (j, 0, 0)),
            pl.BlockSpec((GROUP, WSN // 128, COLS, 128), lambda j: (0, 0, 0, 0)),
        ],
        out_specs=[
            pl.BlockSpec((1, W, R), lambda j: (j, 0, 0)),
            pl.BlockSpec((WSN, R), lambda j: (0, 0)),
        ],
        out_shape=[
            jax.ShapeDtypeStruct((SN_DEV, W, R), bf16),
            jax.ShapeDtypeStruct((WSN, R), bf16),
        ],
        compiler_params=pltpu.CompilerParams(dimension_semantics=("arbitrary",), vmem_limit_bytes=WHOLE),
        name="leaf_backward",
    )(y, pieces, inverse, panels, rows)


def along_leaf(block, distance):
    devices = range(lax.axis_size("leaf"))
    route = [(i - distance, i) for i in devices if i - distance in devices]
    return lax.ppermute(block, "leaf", route)


def hop(block, *chips, cores=(0, 1)):
    return lax.ppermute(block, "sub", [(2 * a + c, 2 * b + c) for a, b in chips for c in cores])


def swap(block, cores=(0, 1)):
    return lax.ppermute(block, "sub", [(2 * HUB + c, 2 * HUB + 1 - c) for c in cores])


def shards(
    leaf_right,
    leaf_inverse,
    panels,
    leaf_subtree,
    panel_block,
    separator_right,
    separator_inverse,
    separator_factor,
):
    section = lax.axis_index("leaf")
    member = lax.axis_index("sub")
    chip, core = member // 2, member % 2
    where = jnp.stack([chip, core, section]).astype(jnp.int32)
    early = [hop(separator_inverse, (k, HUB)) for k in range(3)]
    factors = (separator_factor, swap(separator_factor))
    inverses = (separator_inverse, swap(separator_inverse))
    half = lax.dynamic_slice(separator_factor, (0, 2 * WSN * chip + WSN // 2), (WSN, WSN // 2))
    half = lax.ppermute(half, "sub", [(2 * k + 1, 2 * k) for k in range(3)])
    y, send, *packs = leaf_forward(
        where,
        leaf_subtree,
        panel_block,
        leaf_right,
        leaf_inverse,
        panels,
        separator_right,
        half,
        separator_factor,
    )
    received = lax.all_to_all(send.reshape(GROUP, COLS, SEND), "sub", 0, 0, tiled=True)
    early = [(block, swap(block)) for block in early]
    received, packs, factors, inverses, early = lax.optimization_barrier(
        (received, packs, factors, inverses, early)
    )
    pack2, pack1, pack0 = (hop(block, (k, HUB)) for block, k in zip(packs, (2, 1, 0)))
    base, near, far, slots = scatter(received)
    near, far = along_leaf(near, -1), along_leaf(far, -2)
    pack1 = lax.optimization_barrier((pack1, near, far))[0]
    pack1 = (pack1, swap(pack1))
    near, far, pack0, pack1 = lax.optimization_barrier((near, far, pack0, pack1))
    rhs = (base - near.astype(f32) - far.astype(f32)).astype(bf16)
    pack0 = (pack0, swap(pack0))
    to_hub = [hop(rhs, (k, HUB)) for k in range(3)] + [rhs]
    pack2 = lax.optimization_barrier((pack2, *to_hub[:3], pack0))[0]
    pack2 = (pack2, swap(pack2))
    begun = sweep_head(where, *to_hub, *pack0, *early[0], *pack1, *early[1])
    shares = sweep_rest(
        where, begun, *pack0, *early[0], *pack1, *early[1], *pack2, *early[2], *factors, *inverses
    )
    back = [hop(shares[k], (HUB, k)) for k in range(3)] + [shares[HUB]]
    own = jnp.where(chip == 3, back[3], jnp.where(chip == 2, back[2], jnp.where(chip == 1, back[1], back[0])))
    pieces = extract(slots, own, along_leaf(own, 1), along_leaf(own, 2))
    rows = lax.all_to_all(own.reshape(GROUP, WSN // 128, COLS, 128), "sub", 0, 0, tiled=True)
    pieces = lax.all_to_all(pieces, "sub", 0, 0, tiled=True).reshape(R, UPD)
    return tuple(leaf_backward(y, pieces, leaf_inverse, panels, rows))


def solution(mesh):
    placed = (
        P(("leaf", "sub"), None, None),
        P(("leaf", "sub"), None, None),
        P(("leaf", "sub"), None, None),
        P(("leaf", "sub")),
        P(("leaf", "sub"), None),
        P(("leaf", "sub"), None),
        P(("leaf", "sub"), None),
        P(("leaf", "sub"), None),
    )
    return jax.shard_map(
        shards,
        mesh=mesh,
        in_specs=placed,
        out_specs=(P(("leaf", "sub"), None, None), P(("leaf", "sub"), None)),
        check_vma=False,
    )
```
